512 devices in a mesh: row: 32 (over x_hi, z), col: 16 (over y, x_lo, core).
Axes of the slice: x: 4 (x_hi: 2, x_lo: 2; x = x_hi * 2 + x_lo), y: 4, z: 16, core: 2. Of those that a mesh axis runs over, the one named last changes fastest.
Arguments:
- left: bfloat16 [128, 16384], P('col', 'row'), may hold values from -6 to 6
- right: bfloat16 [128, 16384], P('row', 'col'), may hold values from -6 to 6
- pair_in: bfloat16 [512, 512, 128], P('row', 'col'), may hold values from -6 to 6
- pair_cot: bfloat16 [512, 512, 128], P('row', 'col'), may hold values from -6 to 6
- ln_gain: float32 [128], replicated, may hold values from 0.25 to 1.75
- out_weight: bfloat16 [1024, 128], replicated, may hold values from -2 to 2
- out_bias: float32 [128], replicated, may hold values from -3 to 3
- trans_up: bfloat16 [128, 512], replicated, may hold values from -0.5 to 0.5
- trans_down: bfloat16 [512, 128], replicated, may hold values from -0.25 to 0.25
Outputs:
- pair_out: bfloat16 [512, 512, 128], P('row', 'col')
- grad_left: bfloat16 [128, 16384], P('col', 'row')
- grad_right: bfloat16 [128, 16384], P('row', 'col')
The draws below stay inside these ranges and needn't reach their ends.
All inputs are finite; a program needn't handle non-finite values.
Results may differ from the reference program's by a relative error of at most 0.01.
The reference program's roundings to bfloat16 on the way (of `outer`, `normed`, `hidden`, `d_hidden`, `d_middle` and `d_outer`) count: a program that leaves them out, or rounds other values in their place, can miss the bound.
Values may be sent and summed in bfloat16 or wider, within the bound.
No kernel may reach another device: no remote copies, remote signals or barrier semaphores. Data moves between devices by JAX's collectives and lax.ppermute only.
A program may use at most 64 MiB of HBM per device.

```python
import jax
import jax.numpy as jnp
from jax import lax

C = 32
PAIR = 128
FFN = 512
SEQS = 128
CROP = 512
N_ROW = 32


def block_levels(stream_key, extent, split, least, top_value):
    def one(axis_at, shards_of):
        draws = jax.random.uniform(jax.random.fold_in(jax.random.fold_in(stream_key, 6), axis_at), (shards_of,), jnp.float32, least / len(split), top_value / len(split))
        return jnp.repeat(jnp.exp(draws), extent[axis_at] // shards_of).reshape((-1,) + (1,) * (len(extent) - axis_at - 1))

    level = one(*split[0])
    for cut in split[1:]:
        level = level * one(*cut)
    return level


def bell_draw(rng, extent, width, most, pieces=(), kind=jnp.bfloat16):
    entries = width * jax.random.normal(rng, extent, jnp.float32)
    if pieces:
        entries = entries * block_levels(rng, extent, pieces, -0.22, 0.18)
    return jnp.clip(entries, -most, most).astype(kind)


def setup_inputs(seed: int = 0) -> dict:
    splits = jax.random.split(jax.random.key(seed), 10)
    left = bell_draw(splits[0], (SEQS, CROP * C), 1.0, 6.0, ((0, 16), (1, 32)))
    right = bell_draw(splits[1], (SEQS, CROP * C), 1.0, 6.0, ((0, 32), (1, 16)))
    pair_in = bell_draw(splits[2], (CROP, CROP, PAIR), 1.0, 6.0, ((0, 32), (1, 16)))
    pair_cot = bell_draw(splits[3], (CROP, CROP, PAIR), 1.0, 6.0, ((0, 32), (1, 16)))
    ln_gain = jnp.clip(1.0 + 0.15 * jax.random.normal(splits[4], (PAIR,), jnp.float32), 0.25, 1.75)
    out_weight = bell_draw(splits[5], (C * C, PAIR), (C * C // SEQS) ** -0.5, 2.0)
    out_bias = bell_draw(splits[6], (PAIR,), 0.5, 3.0, (), jnp.float32)
    trans_up = bell_draw(splits[7], (PAIR, FFN), PAIR ** -0.5, 0.5)
    trans_down = bell_draw(splits[8], (FFN, PAIR), FFN ** -0.5, 0.25)
    return dict(left=left, right=right, pair_in=pair_in, pair_cot=pair_cot, ln_gain=ln_gain, out_weight=out_weight, out_bias=out_bias, trans_up=trans_up, trans_down=trans_down)


def pair_block(outer, pair_in, pair_cot, ln_gain, out_weight, out_bias, trans_up, trans_down):
    update = jnp.einsum('ijk,kd->ijd', outer.astype(jnp.float32), out_weight.astype(jnp.float32))
    middle = pair_in.astype(jnp.float32) + update + out_bias
    centre = lax.optimization_barrier(jnp.mean(middle, axis=-1, keepdims=True))
    centred = middle - centre
    spread = lax.optimization_barrier(jnp.mean(centred * centred, axis=-1, keepdims=True))
    inverse = lax.rsqrt(spread + 1e-05)
    normal_x = centred * inverse
    normed = (normal_x * ln_gain).astype(jnp.bfloat16)
    preact = jnp.einsum('ijk,kf->ijf', normed.astype(jnp.float32), trans_up.astype(jnp.float32))
    hidden = jnp.maximum(preact, 0.0).astype(jnp.bfloat16)
    down = jnp.einsum('ijf,fk->ijk', hidden.astype(jnp.float32), trans_down.astype(jnp.float32))
    pair_out = (middle + down).astype(jnp.bfloat16)
    cotangent = pair_cot.astype(jnp.float32)
    back = jnp.einsum('ijk,fk->ijf', cotangent, trans_down.astype(jnp.float32))
    d_hidden = jnp.where(preact > 0.0, back, 0.0).astype(jnp.bfloat16)
    d_normed = jnp.einsum('ijf,kf->ijk', d_hidden.astype(jnp.float32), trans_up.astype(jnp.float32))
    scaled = d_normed * ln_gain
    d_middle = cotangent + inverse * (scaled - lax.optimization_barrier(jnp.mean(scaled, axis=-1, keepdims=True)) - normal_x * lax.optimization_barrier(jnp.mean(scaled * normal_x, axis=-1, keepdims=True)))
    d_middle = d_middle.astype(jnp.bfloat16)
    d_outer = jnp.einsum('ijk,ck->ijc', d_middle.astype(jnp.float32), out_weight.astype(jnp.float32))
    return (pair_out, d_outer.astype(jnp.bfloat16))

def reference(left, right, pair_in, pair_cot, ln_gain, out_weight, out_bias, trans_up, trans_down):
    crop = pair_in.shape[0]
    block = crop // N_ROW
    left_all = left.reshape(SEQS, crop, C).astype(jnp.float32)
    right_all = right.reshape(SEQS, crop, C).astype(jnp.float32)

    def step(carry, index):
        first = (index * block).astype(jnp.int32)
        left_rows = lax.dynamic_slice_in_dim(left_all, first, block, 1)
        pair_rows = lax.dynamic_slice_in_dim(pair_in, first, block, 0)
        cot_rows = lax.dynamic_slice_in_dim(pair_cot, first, block, 0)
        summed = jnp.einsum('sic,sje->ijce', left_rows, right_all)
        outer = (summed * (1.0 / SEQS)).astype(jnp.bfloat16).reshape(block, crop, C * C)
        pair_rows_out, d_outer = pair_block(outer, pair_rows, cot_rows, ln_gain, out_weight, out_bias, trans_up, trans_down)
        grad_tiles = d_outer.reshape(block, crop, C, C).astype(jnp.float32)
        left_grad = jnp.einsum('ijce,sje->sic', grad_tiles, right_all) * (1.0 / SEQS)
        carry = carry + jnp.einsum('ijce,sic->sje', grad_tiles, left_rows)
        return (carry, (pair_rows_out, left_grad.astype(jnp.bfloat16)))
    start_carry = jnp.zeros((SEQS, crop, C), jnp.float32)
    carry, stacked = lax.scan(step, start_carry, jnp.arange(N_ROW, dtype=jnp.int32))
    pair_out = stacked[0].reshape(crop, crop, pair_in.shape[2])
    grad_left = jnp.moveaxis(stacked[1], 0, 1).reshape(SEQS, crop * C)
    grad_right = (carry * (1.0 / SEQS)).astype(jnp.bfloat16).reshape(SEQS, crop * C)
    return (pair_out, grad_left, grad_right)
```

```python
import jax
import jax.numpy as jnp
from jax import lax
from jax.experimental import pallas as pl
from jax.experimental.pallas import tpu as pltpu
from jax.sharding import PartitionSpec as P

C = 32
SEQS = 128
GROUPS = 128 // C
F32 = jnp.float32
BF16 = jnp.bfloat16
NN = (((1,), (0,)), ((), ()))
NT = (((1,), (1,)), ((), ()))
TN = (((0,), (0,)), ((), ()))


def mm(a, b, dims=NN):
    return lax.dot_general(a, b, dims, preferred_element_type=F32)


def swap_rows(major, minor):
    n = major * minor
    row = lax.broadcasted_iota(jnp.int32, (n, n), 0)
    col = lax.broadcasted_iota(jnp.int32, (n, n), 1)
    return jnp.where(col == (row % minor) * major + row // minor, 1.0, 0.0).astype(BF16)


def exchange(tiles):
    axis = tiles[0].ndim - 1
    lane = lax.broadcasted_iota(jnp.int32, tiles[0].shape, axis)
    low, even = lane < 64, lane % 64 < 32
    a0, a1, a2, a3 = tiles
    b0, b2 = jnp.where(low, a0, pltpu.roll(a2, 64, axis)), jnp.where(low, pltpu.roll(a0, 64, axis), a2)
    b1, b3 = jnp.where(low, a1, pltpu.roll(a3, 64, axis)), jnp.where(low, pltpu.roll(a1, 64, axis), a3)
    c0, c1 = jnp.where(even, b0, pltpu.roll(b1, 32, axis)), jnp.where(even, pltpu.roll(b0, 96, axis), b1)
    c2, c3 = jnp.where(even, b2, pltpu.roll(b3, 32, axis)), jnp.where(even, pltpu.roll(b2, 96, axis), b3)
    return c0, c1, c2, c3


def regroup(src, dst, rows, scale=None):
    for g in range(src.shape[0] // (GROUPS * rows)):
        for h in range(src.shape[1] // 128):
            tiles = [
                src[(GROUPS * g + t) * rows : (GROUPS * g + t + 1) * rows, h * 128 : (h + 1) * 128]
                for t in range(GROUPS)
            ]
            if scale is not None:
                tiles = [tile * scale for tile in tiles]
            for t, tile in enumerate(exchange(tiles)):
                at = (GROUPS * h + t) * rows
                dst[at : at + rows, g * 128 : (g + 1) * 128] = tile.astype(dst.dtype)


def prepare(left, pair_in, pair_cot, down, left_t, left_p, pair_p, cot_p, back):
    rows, cols, _ = pair_in.shape
    swap = swap_rows(C, rows)
    swap_pair = swap if cols == C else swap_rows(cols, rows)
    left_t[...] = mm(swap, left[...], NT).astype(BF16)
    left_p[...] = mm(left[...], swap, NT).astype(BF16)
    pair_p[...] = mm(swap_pair, pair_in[...].reshape(rows * cols, -1)).astype(BF16)
    cot = mm(swap_pair, pair_cot[...].reshape(rows * cols, -1)).astype(BF16)
    cot_p[...] = cot
    back[...] = mm(cot, down[...], NT).astype(BF16)


def pair_step(
    right, left_t, left_p, pair_p, cot_p, back, gain, weight, bias, up,
    grad_right, right_all, d_tiles, middle_out, hidden_out,
    tall, outer,
):
    owners, each, width = right.shape
    rows = left_t.shape[0] // C
    for k in range(owners):
        tall[k * each : (k + 1) * each, :] = right[k].astype(F32)
    right_all[...] = tall[: owners * each, :].astype(BF16)
    tall[...] = mm(left_t[...], right_all[...])
    regroup(tall, outer, rows, 1.0 / SEQS)
    middle = pair_p[...].astype(F32) + mm(outer[...], weight[...]) + bias[...]
    middle_out[...] = middle
    centre = jnp.mean(middle, axis=-1, keepdims=True)
    centred = middle - centre
    spread = jnp.mean(centred * centred, axis=-1, keepdims=True)
    inverse = lax.rsqrt(spread + 1e-05)
    normal_x = centred * inverse
    normed = (normal_x * gain[...]).astype(BF16)
    preact = mm(normed, up[...])
    hidden_out[...] = jnp.maximum(preact, 0.0).astype(BF16)
    d_hidden = jnp.where(preact > 0.0, back[...].astype(F32), 0.0).astype(BF16)
    scaled = mm(d_hidden, up[...], NT) * gain[...]
    d_middle = cot_p[...].astype(F32) + inverse * (
        scaled
        - jnp.mean(scaled, axis=-1, keepdims=True)
        - normal_x * jnp.mean(scaled * normal_x, axis=-1, keepdims=True)
    )
    tall[...] = mm(d_middle.astype(BF16), weight[...], NT)
    regroup(tall, d_tiles, rows)
    tall[: owners * each, :] = mm(left_p[...], d_tiles[...])
    for k in range(owners):
        grad_right[k] = tall[k * each : (k + 1) * each, :].astype(BF16)


def finish(right_all, d_tiles, middle, hidden, down, grad_left, pair_out):
    rows, cols, _ = pair_out.shape
    swap = swap_rows(C, rows)
    swap_pair = swap if cols == C else swap_rows(cols, rows)
    partial = mm(right_all[...], d_tiles[...], NT).astype(BF16)
    grad_left[...] = mm(partial, swap).astype(BF16)
    out = (middle[...] + mm(hidden[...], down[...])).astype(BF16)
    pair_out[...] = mm(swap_pair, out, TN).astype(BF16).reshape(pair_out.shape)


def on_core(kernel, outs, scratch=()):
    whole = pl.BlockSpec(memory_space=pltpu.VMEM)

    def run(*args):
        return pl.pallas_call(
            kernel,
            out_shape=[jax.ShapeDtypeStruct(*out) for out in outs],
            in_specs=[whole] * len(args),
            out_specs=[whole] * len(outs),
            scratch_shapes=[pltpu.VMEM(*s) for s in scratch],
            compiler_params=pltpu.CompilerParams(vmem_limit_bytes=32 << 20),
            cost_estimate=pl.CostEstimate(
                flops=400_000_000, bytes_accessed=2_000_000, transcendentals=0
            ),
        )(*args)

    return run


def sent_to_all(shard, axis):
    copies = jnp.broadcast_to(shard, (lax.axis_size(axis), *shard.shape))
    return lax.all_to_all(copies, axis, split_axis=0, concat_axis=0, tiled=True)


def sum_at_owner(tiles, axis):
    arrived = lax.all_to_all(tiles, axis, split_axis=0, concat_axis=0, tiled=True)
    return (arrived.astype(F32).sum(axis=0) * (1.0 / SEQS)).astype(BF16)


def on_device(left, right, pair_in, pair_cot, ln_gain, out_weight, out_bias, trans_up, trans_down):
    rows, cols, dim = pair_in.shape
    cells, ffn = rows * cols, trans_up.shape[1]
    right_blocks = sent_to_all(right, "row")
    left_all = lax.all_gather(left, "col", axis=0, tiled=True)
    left_t, left_p, pair_p, cot_p, back = on_core(
        prepare,
        [
            ((rows * C, SEQS), BF16),
            ((SEQS, rows * C), BF16),
            ((cells, dim), BF16),
            ((cells, dim), BF16),
            ((cells, ffn), BF16),
        ],
    )(left_all, pair_in, pair_cot, trans_down)
    grad_right, right_all, d_tiles, middle, hidden = on_core(
        pair_step,
        [
            (right_blocks.shape, BF16),
            ((SEQS, cols * C), BF16),
            ((rows * C, cols * C), BF16),
            ((cells, dim), F32),
            ((cells, ffn), BF16),
        ],
        [((max(rows * C, cells), cols * C), F32), ((cells, C * C), BF16)],
    )(
        right_blocks, left_t, left_p, pair_p, cot_p, back,
        ln_gain.reshape(1, dim), out_weight, out_bias.reshape(1, dim), trans_up,
    )
    grad_right = sum_at_owner(grad_right, "row")
    grad_left, pair_out = on_core(
        finish, [((SEQS, rows * C), BF16), (pair_in.shape, BF16)]
    )(right_all, d_tiles, middle, hidden, trans_down)
    grad_left = sum_at_owner(grad_left.reshape(-1, *left.shape), "col")
    return pair_out, grad_left, grad_right


def solution(mesh):
    return jax.shard_map(
        on_device,
        mesh=mesh,
        in_specs=(
            P("col", "row"),
            P("row", "col"),
            P("row", "col", None),
            P("row", "col", None),
            P(),
            P(),
            P(),
            P(),
            P(),
        ),
        out_specs=(P("row", "col", None), P("col", "row"), P("row", "col")),
        check_vma=False,
    )
```

```python
import jax
import jax.numpy as jnp
from jax import lax
from jax.experimental import pallas as pl
from jax.experimental.pallas import tpu as pltpu
from jax.sharding import PartitionSpec as P

C = 32
SEQS = 128
GROUPS = 128 // C
F32 = jnp.float32
BF16 = jnp.bfloat16
NN = (((1,), (0,)), ((), ()))
NT = (((1,), (1,)), ((), ()))
TN = (((0,), (0,)), ((), ()))


def mm(a, b, dims=NN):
    return lax.dot_general(a, b, dims, preferred_element_type=F32)


def swap_rows(major, minor):
    n = major * minor
    row = lax.broadcasted_iota(jnp.int32, (n, n), 0)
    col = lax.broadcasted_iota(jnp.int32, (n, n), 1)
    return jnp.where(col == (row % minor) * major + row // minor, 1.0, 0.0).astype(BF16)


def exchange(tiles):
    axis = tiles[0].ndim - 1
    lane = lax.broadcasted_iota(jnp.int32, tiles[0].shape, axis)
    low, even = lane < 64, lane % 64 < 32
    a0, a1, a2, a3 = tiles
    b0, b2 = jnp.where(low, a0, pltpu.roll(a2, 64, axis)), jnp.where(low, pltpu.roll(a0, 64, axis), a2)
    b1, b3 = jnp.where(low, a1, pltpu.roll(a3, 64, axis)), jnp.where(low, pltpu.roll(a1, 64, axis), a3)
    c0, c1 = jnp.where(even, b0, pltpu.roll(b1, 32, axis)), jnp.where(even, pltpu.roll(b0, 96, axis), b1)
    c2, c3 = jnp.where(even, b2, pltpu.roll(b3, 32, axis)), jnp.where(even, pltpu.roll(b2, 96, axis), b3)
    return c0, c1, c2, c3


def regroup(src, dst, rows, scale=None):
    for g in range(src.shape[0] // (GROUPS * rows)):
        for h in range(src.shape[1] // 128):
            tiles = [
                src[(GROUPS * g + t) * rows : (GROUPS * g + t + 1) * rows, h * 128 : (h + 1) * 128]
                for t in range(GROUPS)
            ]
            if scale is not None:
                tiles = [tile * scale for tile in tiles]
            for t, tile in enumerate(exchange(tiles)):
                at = (GROUPS * h + t) * rows
                dst[at : at + rows, g * 128 : (g + 1) * 128] = tile.astype(dst.dtype)


def prepare(
    left, pair_in, pair_cot, down, gain, bias,
    left_t, left_p, pair_p, cot_p, back, gain_out, bias_out,
):
    gain_out[...] = gain[...]
    bias_out[...] = bias[...]
    rows, cols, _ = pair_in.shape
    swap = swap_rows(C, rows)
    swap_pair = swap if cols == C else swap_rows(cols, rows)
    left_t[...] = mm(swap, left[...], NT).astype(BF16)
    left_p[...] = mm(left[...], swap, NT).astype(BF16)
    pair_p[...] = mm(swap_pair, pair_in[...].reshape(rows * cols, -1)).astype(BF16)
    cot = mm(swap_pair, pair_cot[...].reshape(rows * cols, -1)).astype(BF16)
    cot_p[...] = cot
    back[...] = mm(cot, down[...], NT).astype(BF16)


def pair_step(
    right, left_t, left_p, pair_p, cot_p, back, gain, weight, bias, up,
    away, kept, right_all, d_tiles, middle_out, hidden_out,
    tall, outer,
):
    owners, each, width = right.shape
    rows = left_t.shape[0] // C
    for k in range(owners):
        tall[k * each : (k + 1) * each, :] = right[k].astype(F32)
    right_all[...] = tall[: owners * each, :].astype(BF16)
    tall[...] = mm(left_t[...], right_all[...])
    regroup(tall, outer, rows, 1.0 / SEQS)
    middle = pair_p[...].astype(F32) + mm(outer[...], weight[...]) + bias[...]
    middle_out[...] = middle
    centre = jnp.mean(middle, axis=-1, keepdims=True)
    centred = middle - centre
    spread = jnp.mean(centred * centred, axis=-1, keepdims=True)
    inverse = lax.rsqrt(spread + 1e-05)
    normal_x = centred * inverse
    normed = (normal_x * gain[...]).astype(BF16)
    preact = mm(normed, up[...])
    hidden_out[...] = jnp.maximum(preact, 0.0).astype(BF16)
    d_hidden = jnp.where(preact > 0.0, back[...].astype(F32), 0.0).astype(BF16)
    scaled = mm(d_hidden, up[...], NT) * gain[...]
    d_middle = cot_p[...].astype(F32) + inverse * (
        scaled
        - jnp.mean(scaled, axis=-1, keepdims=True)
        - normal_x * jnp.mean(scaled * normal_x, axis=-1, keepdims=True)
    )
    tall[...] = mm(d_middle.astype(BF16), weight[...], NT)
    regroup(tall, d_tiles, rows)
    half = SEQS // 2
    mine = lax.axis_index("row") // (owners // 2)
    away[...] = mm(left_p[pl.ds((1 - mine) * half, half), :], d_tiles[...]).astype(BF16)
    kept[...] = mm(left_p[pl.ds(mine * half, half), :], d_tiles[...])


def left_step(right_all, d_tiles, grad_left):
    partial = mm(right_all[...], d_tiles[...], NT).astype(BF16)
    grad_left[...] = mm(partial, swap_rows(C, grad_left.shape[1] // C)).astype(BF16)


def join_halves(kept, came, tiles, total):
    owners, each, _ = tiles.shape
    total[...] = kept[...] + came[...].astype(F32)
    for k in range(owners):
        tiles[k] = total[k * each : (k + 1) * each, :].astype(BF16)


def finish(middle, hidden, down, pair_out):
    rows, cols, _ = pair_out.shape
    swap_pair = swap_rows(cols, rows)
    out = (middle[...] + mm(hidden[...], down[...])).astype(BF16)
    pair_out[...] = mm(swap_pair, out, TN).astype(BF16).reshape(pair_out.shape)


def on_core(kernel, outs, scratch=()):
    whole = pl.BlockSpec(memory_space=pltpu.VMEM)

    def run(*args):
        return pl.pallas_call(
            kernel,
            out_shape=[jax.ShapeDtypeStruct(*out) for out in outs],
            in_specs=[whole] * len(args),
            out_specs=[whole] * len(outs),
            scratch_shapes=[pltpu.VMEM(*s) for s in scratch],
            compiler_params=pltpu.CompilerParams(vmem_limit_bytes=32 << 20),
            cost_estimate=pl.CostEstimate(
                flops=400_000_000, bytes_accessed=2_000_000, transcendentals=0
            ),
        )(*args)

    return run


def sent_to_all(shard, axis):
    copies = jnp.broadcast_to(shard, (lax.axis_size(axis), *shard.shape))
    return lax.all_to_all(copies, axis, split_axis=0, concat_axis=0, tiled=True)


def sum_at_owner(tiles, axis, groups=None):
    arrived = lax.all_to_all(
        tiles, axis, split_axis=0, concat_axis=0, tiled=True, axis_index_groups=groups
    )
    return (arrived.astype(F32).sum(axis=0) * (1.0 / SEQS)).astype(BF16)


def on_device(left, right, pair_in, pair_cot, ln_gain, out_weight, out_bias, trans_up, trans_down):
    rows, cols, dim = pair_in.shape
    cells, ffn = rows * cols, trans_up.shape[1]
    right_blocks = sent_to_all(right, "row")
    left_all = lax.all_gather(left, "col", axis=0, tiled=True)
    left_t, left_p, pair_p, cot_p, back, gain, bias = on_core(
        prepare,
        [
            ((rows * C, SEQS), BF16),
            ((SEQS, rows * C), BF16),
            ((cells, dim), BF16),
            ((cells, dim), BF16),
            ((cells, ffn), BF16),
            ((1, dim), F32),
            ((1, dim), F32),
        ],
    )(
        left_all, pair_in, pair_cot, trans_down,
        ln_gain.reshape(1, dim), out_bias.reshape(1, dim),
    )
    away, kept, right_all, d_tiles, middle, hidden = on_core(
        pair_step,
        [
            ((SEQS // 2, cols * C), BF16),
            ((SEQS // 2, cols * C), F32),
            ((SEQS, cols * C), BF16),
            ((rows * C, cols * C), BF16),
            ((cells, dim), F32),
            ((cells, ffn), BF16),
        ],
        [((max(rows * C, cells), cols * C), F32), ((cells, C * C), BF16)],
    )(right_blocks, left_t, left_p, pair_p, cot_p, back, gain, out_weight, bias, trans_up)
    owners = lax.axis_size("row")
    half = owners // 2
    came = lax.ppermute(away, "row", [(k, (k + half) % owners) for k in range(owners)])
    (grad_left,) = on_core(left_step, [((SEQS, rows * C), BF16)])(right_all, d_tiles)
    grad_left = sum_at_owner(grad_left.reshape(-1, *left.shape), "col")
    (tiles,) = on_core(
        join_halves, [((half, *right.shape), BF16)], [((SEQS // 2, cols * C), F32)]
    )(kept, came)
    grad_right = sum_at_owner(
        tiles, "row", [list(range(half)), list(range(half, owners))]
    )
    (pair_out,) = on_core(finish, [(pair_in.shape, BF16)])(middle, hidden, trans_down)
    return pair_out, grad_left, grad_right


def solution(mesh):
    return jax.shard_map(
        on_device,
        mesh=mesh,
        in_specs=(
            P("col", "row"),
            P("row", "col"),
            P("row", "col", None),
            P("row", "col", None),
            P(),
            P(),
            P(),
            P(),
            P(),
        ),
        out_specs=(P("row", "col", None), P("col", "row"), P("row", "col")),
        check_vma=False,
    )
```

```python
import jax
import jax.numpy as jnp
from jax import lax
from jax.experimental import pallas as pl
from jax.experimental.pallas import tpu as pltpu
from jax.sharding import PartitionSpec as P

C = 32
SEQS = 128
GROUPS = 128 // C
F32 = jnp.float32
BF16 = jnp.bfloat16
FIRST = 11
NN = (((1,), (0,)), ((), ()))
NT = (((1,), (1,)), ((), ()))
TN = (((0,), (0,)), ((), ()))


def mm(a, b, dims=NN):
    return lax.dot_general(a, b, dims, preferred_element_type=F32)


def swap_rows(major, minor):
    n = major * minor
    row = lax.broadcasted_iota(jnp.int32, (n, n), 0)
    col = lax.broadcasted_iota(jnp.int32, (n, n), 1)
    return jnp.where(col == (row % minor) * major + row // minor, 1.0, 0.0).astype(BF16)


def exchange(tiles):
    axis = tiles[0].ndim - 1
    lane = lax.broadcasted_iota(jnp.int32, tiles[0].shape, axis)
    low, even = lane < 64, lane % 64 < 32
    a0, a1, a2, a3 = tiles
    b0, b2 = jnp.where(low, a0, pltpu.roll(a2, 64, axis)), jnp.where(low, pltpu.roll(a0, 64, axis), a2)
    b1, b3 = jnp.where(low, a1, pltpu.roll(a3, 64, axis)), jnp.where(low, pltpu.roll(a1, 64, axis), a3)
    c0, c1 = jnp.where(even, b0, pltpu.roll(b1, 32, axis)), jnp.where(even, pltpu.roll(b0, 96, axis), b1)
    c2, c3 = jnp.where(even, b2, pltpu.roll(b3, 32, axis)), jnp.where(even, pltpu.roll(b2, 96, axis), b3)
    return c0, c1, c2, c3


def regroup(src, dst, rows, scale=None):
    for g in range(src.shape[0] // (GROUPS * rows)):
        for h in range(src.shape[1] // 128):
            tiles = [
                src[(GROUPS * g + t) * rows : (GROUPS * g + t + 1) * rows, h * 128 : (h + 1) * 128]
                for t in range(GROUPS)
            ]
            if scale is not None:
                tiles = [tile * scale for tile in tiles]
            for t, tile in enumerate(exchange(tiles)):
                at = (GROUPS * h + t) * rows
                dst[at : at + rows, g * 128 : (g + 1) * 128] = tile.astype(dst.dtype)


def prepare(left, pair_in, pair_cot, down, left_t, left_p, pair_p, cot_p, back):
    rows, cols, _ = pair_in.shape
    swap = swap_rows(C, rows)
    swap_pair = swap if cols == C else swap_rows(cols, rows)
    left_t[...] = mm(swap, left[...], NT).astype(BF16)
    left_p[...] = mm(left[...], swap, NT).astype(BF16)
    pair_p[...] = mm(swap_pair, pair_in[...].reshape(rows * cols, -1)).astype(BF16)
    cot = mm(swap_pair, pair_cot[...].reshape(rows * cols, -1)).astype(BF16)
    cot_p[...] = cot
    back[...] = mm(cot, down[...], NT).astype(BF16)


def from_first(count):
    return [(FIRST + k) % count for k in range(count)]


def pair_step(
    right, left_t, left_p, pair_p, cot_p, back, weight, up, gain_in, bias_in,
    away, kept, middle_out, hidden_out, grad_left,
    tall, outer, right_all, d_tiles, partial, gain, bias, sems,
):
    fetch_gain = pltpu.make_async_copy(gain_in, gain, sems.at[0])
    fetch_bias = pltpu.make_async_copy(bias_in, bias, sems.at[1])
    fetch_gain.start()
    fetch_bias.start()
    owners, each, width = right.shape
    rows = left_t.shape[0] // C
    for k, z in enumerate(from_first(owners // 2)):
        for at, block in ((z, k), (z + owners // 2, k + owners // 2)):
            tall[at * each : (at + 1) * each, :] = right[block].astype(F32)
    right_all[...] = tall[: owners * each, :].astype(BF16)
    tall[...] = mm(left_t[...], right_all[...])
    regroup(tall, outer, rows, 1.0 / SEQS)
    update = mm(outer[...], weight[...])
    fetch_gain.wait()
    fetch_bias.wait()
    middle = pair_p[...].astype(F32) + update + bias[...]
    middle_out[...] = middle
    centre = jnp.mean(middle, axis=-1, keepdims=True)
    centred = middle - centre
    spread = jnp.mean(centred * centred, axis=-1, keepdims=True)
    inverse = lax.rsqrt(spread + 1e-05)
    normal_x = centred * inverse
    normed = (normal_x * gain[...]).astype(BF16)
    preact = mm(normed, up[...])
    hidden_out[...] = jnp.maximum(preact, 0.0).astype(BF16)
    d_hidden = jnp.where(preact > 0.0, back[...].astype(F32), 0.0).astype(BF16)
    scaled = mm(d_hidden, up[...], NT) * gain[...]
    d_middle = cot_p[...].astype(F32) + inverse * (
        scaled
        - jnp.mean(scaled, axis=-1, keepdims=True)
        - normal_x * jnp.mean(scaled * normal_x, axis=-1, keepdims=True)
    )
    tall[...] = mm(d_middle.astype(BF16), weight[...], NT)
    regroup(tall, d_tiles, rows)
    partial[...] = mm(right_all[...], d_tiles[...], NT).astype(BF16)
    send = pltpu.make_async_copy(partial, grad_left, sems.at[2])
    send.start()
    half = SEQS // 2
    mine = lax.axis_index("row") // (owners // 2)
    away[...] = mm(left_p[pl.ds((1 - mine) * half, half), :], d_tiles[...]).astype(BF16)
    kept[...] = mm(left_p[pl.ds(mine * half, half), :], d_tiles[...])
    send.wait()


def left_sum(arrived, grad_left):
    total = jnp.sum(arrived[...].astype(F32), axis=0)
    mine = (total * (1.0 / SEQS)).astype(BF16)
    grad_left[...] = mm(mine, swap_rows(C, grad_left.shape[1] // C)).astype(BF16)


def right_sum(arrived, grad_right):
    total = jnp.sum(arrived[...].astype(F32), axis=0)
    grad_right[...] = (total * (1.0 / SEQS)).astype(BF16)


def join_halves(kept, came, tiles, total):
    owners, each, _ = tiles.shape
    total[...] = kept[...] + came[...].astype(F32)
    for k, z in enumerate(from_first(owners)):
        tiles[k] = total[z * each : (z + 1) * each, :].astype(BF16)


def finish(middle, hidden, down, pair_out):
    rows, cols, _ = pair_out.shape
    swap_pair = swap_rows(cols, rows)
    out = (middle[...] + mm(hidden[...], down[...])).astype(BF16)
    pair_out[...] = mm(swap_pair, out, TN).astype(BF16).reshape(pair_out.shape)


def in_hbm(x):
    return pltpu.with_memory_space_constraint(x, pltpu.HBM)


VMEM = pl.BlockSpec(memory_space=pltpu.VMEM)
HBM = pl.BlockSpec(memory_space=pltpu.HBM)


def on_core(kernel, args, outs, scratch=(), far_in=0, far_out=0):
    return pl.pallas_call(
        kernel,
        out_shape=[jax.ShapeDtypeStruct(*out) for out in outs],
        in_specs=[VMEM] * (len(args) - far_in) + [HBM] * far_in,
        out_specs=[VMEM] * (len(outs) - far_out) + [HBM] * far_out,
        scratch_shapes=[pltpu.VMEM(*s) if isinstance(s, tuple) else s for s in scratch],
        compiler_params=pltpu.CompilerParams(vmem_limit_bytes=32 << 20),
        cost_estimate=pl.CostEstimate(
            flops=400_000_000, bytes_accessed=2_000_000, transcendentals=0
        ),
    )(*args)


def to_each(tiles, axis, groups=None):
    return lax.all_to_all(
        tiles, axis, split_axis=0, concat_axis=0, tiled=True, axis_index_groups=groups
    )


def on_device(left, right, pair_in, pair_cot, ln_gain, out_weight, out_bias, trans_up, trans_down):
    rows, cols, dim = pair_in.shape
    cells, ffn = rows * cols, trans_up.shape[1]
    left_size, right_size = rows * C, cols * C
    owners = lax.axis_size("row")
    half = owners // 2
    halves = [[start + z for z in from_first(half)] for start in (0, half)]
    copies = jnp.broadcast_to(right, (owners, *right.shape))
    right_blocks = to_each(copies, "row", [halves[0] + halves[1]])
    left_all = lax.all_gather(left, "col", axis=0, tiled=True)
    left_t, left_p, pair_p, cot_p, back = on_core(
        prepare,
        [left_all, pair_in, pair_cot, trans_down],
        [
            ((left_size, SEQS), BF16),
            ((SEQS, left_size), BF16),
            ((cells, dim), BF16),
            ((cells, dim), BF16),
            ((cells, ffn), BF16),
        ],
    )
    away, kept, middle, hidden, grad_left = on_core(
        pair_step,
        [
            right_blocks, left_t, left_p, pair_p, cot_p, back, out_weight, trans_up,
            in_hbm(ln_gain.reshape(1, dim)), in_hbm(out_bias.reshape(1, dim)),
        ],
        [
            ((SEQS // 2, right_size), BF16),
            ((SEQS // 2, right_size), F32),
            ((cells, dim), F32),
            ((cells, ffn), BF16),
            ((SEQS, left_size), BF16),
        ],
        [
            ((max(left_size, cells), max(right_size, C * C)), F32),
            ((cells, C * C), BF16),
            ((SEQS, right_size), BF16),
            ((left_size, right_size), BF16),
            ((SEQS, left_size), BF16),
            ((1, dim), F32),
            ((1, dim), F32),
            pltpu.SemaphoreType.DMA((3,)),
        ],
        far_in=2,
        far_out=1,
    )
    came = lax.ppermute(away, "row", [(k, (k + half) % owners) for k in range(owners)])
    left_tiles = to_each(grad_left.reshape(-1, *left.shape), "col")
    (tiles,) = on_core(
        join_halves, [kept, came], [((half, *right.shape), BF16)], [((SEQS // 2, right_size), F32)]
    )
    right_tiles = to_each(tiles, "row", halves)
    (pair_out,) = on_core(finish, [middle, hidden, trans_down], [(pair_in.shape, BF16)])
    (grad_left,) = on_core(left_sum, [left_tiles], [(left.shape, BF16)])
    (grad_right,) = on_core(right_sum, [right_tiles], [(right.shape, BF16)])
    return pair_out, grad_left, grad_right


def solution(mesh):
    return jax.shard_map(
        on_device,
        mesh=mesh,
        in_specs=(
            P("col", "row"),
            P("row", "col"),
            P("row", "col", None),
            P("row", "col", None),
            P(),
            P(),
            P(),
            P(),
            P(),
        ),
        out_specs=(P("row", "col", None), P("col", "row"), P("row", "col")),
        check_vma=False,
    )
```

```python
import jax
import jax.numpy as jnp
from jax import lax
from jax.experimental import pallas as pl
from jax.experimental.pallas import tpu as pltpu
from jax.sharding import PartitionSpec as P

C = 32
SEQS = 128
GROUPS = 128 // C
F32 = jnp.float32
BF16 = jnp.bfloat16
Y, X, CORES = 4, 2, 2
FIRST = 11
NN = (((1,), (0,)), ((), ()))
NT = (((1,), (1,)), ((), ()))
TN = (((0,), (0,)), ((), ()))


def mm(a, b, dims=NN):
    return lax.dot_general(a, b, dims, preferred_element_type=F32)


def swap_rows(major, minor):
    n = major * minor
    row = lax.broadcasted_iota(jnp.int32, (n, n), 0)
    col = lax.broadcasted_iota(jnp.int32, (n, n), 1)
    return jnp.where(col == (row % minor) * major + row // minor, 1.0, 0.0).astype(BF16)


def exchange(tiles):
    axis = tiles[0].ndim - 1
    lane = lax.broadcasted_iota(jnp.int32, tiles[0].shape, axis)
    low, even = lane < 64, lane % 64 < 32
    a0, a1, a2, a3 = tiles
    b0, b2 = jnp.where(low, a0, pltpu.roll(a2, 64, axis)), jnp.where(low, pltpu.roll(a0, 64, axis), a2)
    b1, b3 = jnp.where(low, a1, pltpu.roll(a3, 64, axis)), jnp.where(low, pltpu.roll(a1, 64, axis), a3)
    c0, c1 = jnp.where(even, b0, pltpu.roll(b1, 32, axis)), jnp.where(even, pltpu.roll(b0, 96, axis), b1)
    c2, c3 = jnp.where(even, b2, pltpu.roll(b3, 32, axis)), jnp.where(even, pltpu.roll(b2, 96, axis), b3)
    return c0, c1, c2, c3


def regroup(src, dst, rows, scale=None):
    for g in range(src.shape[0] // (GROUPS * rows)):
        for h in range(src.shape[1] // 128):
            tiles = [
                src[(GROUPS * g + t) * rows : (GROUPS * g + t + 1) * rows, h * 128 : (h + 1) * 128]
                for t in range(GROUPS)
            ]
            if scale is not None:
                tiles = [tile * scale for tile in tiles]
            for t, tile in enumerate(exchange(tiles)):
                at = (GROUPS * h + t) * rows
                dst[at : at + rows, g * 128 : (g + 1) * 128] = tile.astype(dst.dtype)


def prepare(left, pair_in, pair_cot, down, left_t, left_p, pair_p, cot_p, back):
    rows, cols, _ = pair_in.shape
    swap = swap_rows(C, rows)
    swap_pair = swap if cols == C else swap_rows(cols, rows)
    ring = chip_ring()
    each = left.shape[0] // len(ring)
    came = left[...].astype(F32)
    blocks = [came[ring.index(k) * each : (ring.index(k) + 1) * each] for k in range(len(ring))]
    left_all = jnp.concatenate(blocks, axis=0).astype(BF16)
    left_t[...] = mm(swap, left_all, NT).astype(BF16)
    left_p[...] = mm(left_all, swap, NT).astype(BF16)
    pair_p[...] = mm(swap_pair, pair_in[...].reshape(rows * cols, -1)).astype(BF16)
    cot = mm(swap_pair, pair_cot[...].reshape(rows * cols, -1)).astype(BF16)
    cot_p[...] = cot
    back[...] = mm(cot, down[...], NT).astype(BF16)


def chip_ring():
    chips = [(y, 0) for y in range(Y)] + [(y, 1) for y in reversed(range(Y))]
    return [(y * X + x) * CORES + core for y, x in chips for core in range(CORES)]


def from_first(count):
    return [(FIRST + k) % count for k in range(count)]


def pair_step(
    right, left_t, left_p, pair_p, cot_p, back, weight, up, gain_in, bias_in,
    away, kept, middle_out, hidden_out, grad_left,
    tall, outer, right_all, d_tiles, partial, gain, bias, sems,
):
    fetch_gain = pltpu.make_async_copy(gain_in, gain, sems.at[0])
    fetch_bias = pltpu.make_async_copy(bias_in, bias, sems.at[1])
    fetch_gain.start()
    fetch_bias.start()
    owners, each, width = right.shape
    rows = left_t.shape[0] // C
    for k, z in enumerate(from_first(owners // 2)):
        for at, block in ((z, k), (z + owners // 2, k + owners // 2)):
            tall[at * each : (at + 1) * each, :] = right[block].astype(F32)
    right_all[...] = tall[: owners * each, :].astype(BF16)
    tall[...] = mm(left_t[...], right_all[...])
    regroup(tall, outer, rows, 1.0 / SEQS)
    update = mm(outer[...], weight[...])
    fetch_gain.wait()
    fetch_bias.wait()
    middle = pair_p[...].astype(F32) + update + bias[...]
    middle_out[...] = middle
    centre = jnp.mean(middle, axis=-1, keepdims=True)
    centred = middle - centre
    spread = jnp.mean(centred * centred, axis=-1, keepdims=True)
    inverse = lax.rsqrt(spread + 1e-05)
    normal_x = centred * inverse
    normed = (normal_x * gain[...]).astype(BF16)
    preact = mm(normed, up[...])
    hidden_out[...] = jnp.maximum(preact, 0.0).astype(BF16)
    d_hidden = jnp.where(preact > 0.0, back[...].astype(F32), 0.0).astype(BF16)
    scaled = mm(d_hidden, up[...], NT) * gain[...]
    d_middle = cot_p[...].astype(F32) + inverse * (
        scaled
        - jnp.mean(scaled, axis=-1, keepdims=True)
        - normal_x * jnp.mean(scaled * normal_x, axis=-1, keepdims=True)
    )
    tall[...] = mm(d_middle.astype(BF16), weight[...], NT)
    regroup(tall, d_tiles, rows)
    partial[...] = mm(right_all[...], d_tiles[...], NT).astype(BF16)
    send = pltpu.make_async_copy(partial, grad_left, sems.at[2])
    send.start()
    half = SEQS // 2
    mine = lax.axis_index("row") // (owners // 2)
    away[...] = mm(left_p[pl.ds((1 - mine) * half, half), :], d_tiles[...]).astype(BF16)
    kept[...] = mm(left_p[pl.ds(mine * half, half), :], d_tiles[...])
    send.wait()


def left_sum(arrived, grad_left):
    total = jnp.sum(arrived[...].astype(F32), axis=0)
    mine = (total * (1.0 / SEQS)).astype(BF16)
    grad_left[...] = mm(mine, swap_rows(C, grad_left.shape[1] // C)).astype(BF16)


def right_sum(arrived, grad_right):
    total = jnp.sum(arrived[...].astype(F32), axis=0)
    grad_right[...] = (total * (1.0 / SEQS)).astype(BF16)


def join_halves(kept, came, tiles, total):
    owners, each, _ = tiles.shape
    total[...] = kept[...] + came[...].astype(F32)
    for k, z in enumerate(from_first(owners)):
        tiles[k] = total[z * each : (z + 1) * each, :].astype(BF16)


def finish(middle, hidden, down, pair_out):
    rows, cols, _ = pair_out.shape
    swap_pair = swap_rows(cols, rows)
    out = (middle[...] + mm(hidden[...], down[...])).astype(BF16)
    pair_out[...] = mm(swap_pair, out, TN).astype(BF16).reshape(pair_out.shape)


def in_hbm(x):
    return pltpu.with_memory_space_constraint(x, pltpu.HBM)


VMEM = pl.BlockSpec(memory_space=pltpu.VMEM)
HBM = pl.BlockSpec(memory_space=pltpu.HBM)


def on_core(kernel, args, outs, scratch=(), far_in=0, far_out=0):
    return pl.pallas_call(
        kernel,
        out_shape=[jax.ShapeDtypeStruct(*out) for out in outs],
        in_specs=[VMEM] * (len(args) - far_in) + [HBM] * far_in,
        out_specs=[VMEM] * (len(outs) - far_out) + [HBM] * far_out,
        scratch_shapes=[pltpu.VMEM(*s) if isinstance(s, tuple) else s for s in scratch],
        compiler_params=pltpu.CompilerParams(vmem_limit_bytes=32 << 20),
        cost_estimate=pl.CostEstimate(
            flops=400_000_000, bytes_accessed=2_000_000, transcendentals=0
        ),
    )(*args)


def to_each(tiles, axis, groups=None):
    return lax.all_to_all(
        tiles, axis, split_axis=0, concat_axis=0, tiled=True, axis_index_groups=groups
    )


def on_device(left, right, pair_in, pair_cot, ln_gain, out_weight, out_bias, trans_up, trans_down):
    rows, cols, dim = pair_in.shape
    cells, ffn = rows * cols, trans_up.shape[1]
    left_size, right_size = rows * C, cols * C
    owners = lax.axis_size("row")
    half = owners // 2
    halves = [[start + z for z in from_first(half)] for start in (0, half)]
    copies = jnp.broadcast_to(right, (owners, *right.shape))
    right_blocks = to_each(copies, "row", [halves[0] + halves[1]])
    left_blocks = lax.all_gather(
        left, "col", axis=0, tiled=True, axis_index_groups=[chip_ring()]
    )
    left_t, left_p, pair_p, cot_p, back = on_core(
        prepare,
        [left_blocks, pair_in, pair_cot, trans_down],
        [
            ((left_size, SEQS), BF16),
            ((SEQS, left_size), BF16),
            ((cells, dim), BF16),
            ((cells, dim), BF16),
            ((cells, ffn), BF16),
        ],
    )
    away, kept, middle, hidden, grad_left = on_core(
        pair_step,
        [
            right_blocks, left_t, left_p, pair_p, cot_p, back, out_weight, trans_up,
            in_hbm(ln_gain.reshape(1, dim)), in_hbm(out_bias.reshape(1, dim)),
        ],
        [
            ((SEQS // 2, right_size), BF16),
            ((SEQS // 2, right_size), F32),
            ((cells, dim), F32),
            ((cells, ffn), BF16),
            ((SEQS, left_size), BF16),
        ],
        [
            ((max(left_size, cells), max(right_size, C * C)), F32),
            ((cells, C * C), BF16),
            ((SEQS, right_size), BF16),
            ((left_size, right_size), BF16),
            ((SEQS, left_size), BF16),
            ((1, dim), F32),
            ((1, dim), F32),
            pltpu.SemaphoreType.DMA((3,)),
        ],
        far_in=2,
        far_out=1,
    )
    came = lax.ppermute(away, "row", [(k, (k + half) % owners) for k in range(owners)])
    left_tiles = to_each(grad_left.reshape(-1, *left.shape), "col")
    (tiles,) = on_core(
        join_halves, [kept, came], [((half, *right.shape), BF16)], [((SEQS // 2, right_size), F32)]
    )
    right_tiles = to_each(tiles, "row", halves)
    (pair_out,) = on_core(finish, [middle, hidden, trans_down], [(pair_in.shape, BF16)])
    (grad_left,) = on_core(left_sum, [left_tiles], [(left.shape, BF16)])
    (grad_right,) = on_core(right_sum, [right_tiles], [(right.shape, BF16)])
    return pair_out, grad_left, grad_right


def solution(mesh):
    return jax.shard_map(
        on_device,
        mesh=mesh,
        in_specs=(
            P("col", "row"),
            P("row", "col"),
            P("row", "col", None),
            P("row", "col", None),
            P(),
            P(),
            P(),
            P(),
            P(),
        ),
        out_specs=(P("row", "col", None), P("col", "row"), P("row", "col")),
        check_vma=False,
    )
```

```python
import jax
import jax.numpy as jnp
from jax import lax
from jax.experimental import pallas as pl
from jax.experimental.pallas import tpu as pltpu
from jax.sharding import PartitionSpec as P

C = 32
SEQS = 128
GROUPS = 128 // C
F32 = jnp.float32
BF16 = jnp.bfloat16
Y, X, CORES = 4, 2, 2
OUT, BACK = (11, 1), (8, 7)
NN = (((1,), (0,)), ((), ()))
NT = (((1,), (1,)), ((), ()))
TN = (((0,), (0,)), ((), ()))


def mm(a, b, dims=NN):
    return lax.dot_general(a, b, dims, preferred_element_type=F32)


def swap_rows(major, minor):
    n = major * minor
    row = lax.broadcasted_iota(jnp.int32, (n, n), 0)
    col = lax.broadcasted_iota(jnp.int32, (n, n), 1)
    return jnp.where(col == (row % minor) * major + row // minor, 1.0, 0.0).astype(BF16)


def exchange(tiles):
    axis = tiles[0].ndim - 1
    lane = lax.broadcasted_iota(jnp.int32, tiles[0].shape, axis)
    low, even = lane < 64, lane % 64 < 32
    a0, a1, a2, a3 = tiles
    b0, b2 = jnp.where(low, a0, pltpu.roll(a2, 64, axis)), jnp.where(low, pltpu.roll(a0, 64, axis), a2)
    b1, b3 = jnp.where(low, a1, pltpu.roll(a3, 64, axis)), jnp.where(low, pltpu.roll(a1, 64, axis), a3)
    c0, c1 = jnp.where(even, b0, pltpu.roll(b1, 32, axis)), jnp.where(even, pltpu.roll(b0, 96, axis), b1)
    c2, c3 = jnp.where(even, b2, pltpu.roll(b3, 32, axis)), jnp.where(even, pltpu.roll(b2, 96, axis), b3)
    return c0, c1, c2, c3


def regroup(src, dst, rows, scale=None):
    for g in range(src.shape[0] // (GROUPS * rows)):
        for h in range(src.shape[1] // 128):
            tiles = [
                src[(GROUPS * g + t) * rows : (GROUPS * g + t + 1) * rows, h * 128 : (h + 1) * 128]
                for t in range(GROUPS)
            ]
            if scale is not None:
                tiles = [tile * scale for tile in tiles]
            tiles = [tile.astype(BF16) for tile in tiles]
            for t, tile in enumerate(exchange(tiles)):
                at = (GROUPS * h + t) * rows
                dst[at : at + rows, g * 128 : (g + 1) * 128] = tile


def prepare(left, pair_in, pair_cot, down, left_t, left_p, pair_p, cot_p, back):
    rows, cols, _ = pair_in.shape
    swap = swap_rows(C, rows)
    swap_pair = swap if cols == C else swap_rows(cols, rows)
    ring = chip_ring()
    each = left.shape[0] // len(ring)
    came = left[...].astype(F32)
    blocks = [came[ring.index(k) * each : (ring.index(k) + 1) * each] for k in range(len(ring))]
    left_all = jnp.concatenate(blocks, axis=0).astype(BF16)
    left_t[...] = mm(swap, left_all, NT).astype(BF16)
    left_p[...] = mm(left_all, swap, NT).astype(BF16)
    pair_p[...] = mm(swap_pair, pair_in[...].reshape(rows * cols, -1)).astype(BF16)
    cot = mm(swap_pair, pair_cot[...].reshape(rows * cols, -1)).astype(BF16)
    cot_p[...] = cot
    back[...] = mm(cot, down[...], NT).astype(BF16)


def chip_ring():
    chips = [(y, 0) for y in range(Y)] + [(y, 1) for y in reversed(range(Y))]
    return [(y * X + x) * CORES + core for y, x in chips for core in range(CORES)]


def listed(count, order):
    first, stride = order
    return [(first + stride * k) % count for k in range(count)]


def pair_step(
    right, left_t, left_p, pair_p, cot_p, back, weight, up, gain_in, bias_in,
    away, kept, middle_out, hidden_out, grad_left,
    tall, outer, right_all, d_tiles, partial, gain, bias, sems,
):
    fetch_gain = pltpu.make_async_copy(gain_in, gain, sems.at[0])
    fetch_bias = pltpu.make_async_copy(bias_in, bias, sems.at[1])
    fetch_gain.start()
    fetch_bias.start()
    owners, each, width = right.shape
    rows = left_t.shape[0] // C
    for k, z in enumerate(listed(owners // 2, OUT)):
        for at, block in ((z, k), (z + owners // 2, k + owners // 2)):
            tall[at * each : (at + 1) * each, :] = right[block].astype(F32)
    right_all[...] = tall[: owners * each, :].astype(BF16)
    tall[...] = mm(left_t[...], right_all[...])
    regroup(tall, outer, rows, 1.0 / SEQS)
    update = mm(outer[...], weight[...])
    fetch_gain.wait()
    fetch_bias.wait()
    middle = pair_p[...].astype(F32) + update + bias[...]
    middle_out[...] = middle
    centre = jnp.mean(middle, axis=-1, keepdims=True)
    centred = middle - centre
    spread = jnp.mean(centred * centred, axis=-1, keepdims=True)
    inverse = lax.rsqrt(spread + 1e-05)
    normal_x = centred * inverse
    normed = (normal_x * gain[...]).astype(BF16)
    preact = mm(normed, up[...])
    hidden_out[...] = jnp.maximum(preact, 0.0).astype(BF16)
    d_hidden = jnp.where(preact > 0.0, back[...].astype(F32), 0.0).astype(BF16)
    scaled = mm(d_hidden, up[...], NT) * gain[...]
    d_middle = cot_p[...].astype(F32) + inverse * (
        scaled
        - jnp.mean(scaled, axis=-1, keepdims=True)
        - normal_x * jnp.mean(scaled * normal_x, axis=-1, keepdims=True)
    )
    tall[...] = mm(d_middle.astype(BF16), weight[...], NT)
    regroup(tall, d_tiles, rows)
    partial[...] = mm(right_all[...], d_tiles[...], NT).astype(BF16)
    send = pltpu.make_async_copy(partial, grad_left, sems.at[2])
    send.start()
    half = SEQS // 2
    mine = lax.axis_index("row") // (owners // 2)
    away[...] = mm(left_p[pl.ds((1 - mine) * half, half), :], d_tiles[...]).astype(BF16)
    kept[...] = mm(left_p[pl.ds(mine * half, half), :], d_tiles[...])
    send.wait()


def left_sum(arrived, grad_left):
    total = jnp.sum(arrived[...].astype(F32), axis=0)
    mine = (total * (1.0 / SEQS)).astype(BF16)
    grad_left[...] = mm(mine, swap_rows(C, grad_left.shape[1] // C)).astype(BF16)


def right_sum(arrived, grad_right):
    total = jnp.sum(arrived[...].astype(F32), axis=0)
    grad_right[...] = (total * (1.0 / SEQS)).astype(BF16)


def join_halves(kept, came, tiles, total):
    owners, each, _ = tiles.shape
    total[...] = kept[...] + came[...].astype(F32)
    for k, z in enumerate(listed(owners, BACK)):
        tiles[k] = total[z * each : (z + 1) * each, :].astype(BF16)


def finish(middle, hidden, down, pair_out):
    rows, cols, _ = pair_out.shape
    swap_pair = swap_rows(cols, rows)
    out = (middle[...] + mm(hidden[...], down[...])).astype(BF16)
    pair_out[...] = mm(swap_pair, out, TN).astype(BF16).reshape(pair_out.shape)


def in_hbm(x):
    return pltpu.with_memory_space_constraint(x, pltpu.HBM)


VMEM = pl.BlockSpec(memory_space=pltpu.VMEM)
HBM = pl.BlockSpec(memory_space=pltpu.HBM)


def on_core(kernel, args, outs, scratch=(), far_in=0, far_out=0):
    return pl.pallas_call(
        kernel,
        out_shape=[jax.ShapeDtypeStruct(*out) for out in outs],
        in_specs=[VMEM] * (len(args) - far_in) + [HBM] * far_in,
        out_specs=[VMEM] * (len(outs) - far_out) + [HBM] * far_out,
        scratch_shapes=[pltpu.VMEM(*s) if isinstance(s, tuple) else s for s in scratch],
        compiler_params=pltpu.CompilerParams(vmem_limit_bytes=32 << 20),
        cost_estimate=pl.CostEstimate(
            flops=400_000_000, bytes_accessed=2_000_000, transcendentals=0
        ),
    )(*args)


def to_each(tiles, axis, groups=None):
    return lax.all_to_all(
        tiles, axis, split_axis=0, concat_axis=0, tiled=True, axis_index_groups=groups
    )


def on_device(left, right, pair_in, pair_cot, ln_gain, out_weight, out_bias, trans_up, trans_down):
    rows, cols, dim = pair_in.shape
    cells, ffn = rows * cols, trans_up.shape[1]
    left_size, right_size = rows * C, cols * C
    owners = lax.axis_size("row")
    half = owners // 2
    out_order, back_order = (
        [[start + z for z in listed(half, order)] for start in (0, half)] for order in (OUT, BACK)
    )
    copies = jnp.broadcast_to(right, (owners, *right.shape))
    right_blocks = to_each(copies, "row", [out_order[0] + out_order[1]])
    left_blocks = lax.all_gather(
        left, "col", axis=0, tiled=True, axis_index_groups=[chip_ring()]
    )
    left_t, left_p, pair_p, cot_p, back = on_core(
        prepare,
        [left_blocks, pair_in, pair_cot, trans_down],
        [
            ((left_size, SEQS), BF16),
            ((SEQS, left_size), BF16),
            ((cells, dim), BF16),
            ((cells, dim), BF16),
            ((cells, ffn), BF16),
        ],
    )
    away, kept, middle, hidden, grad_left = on_core(
        pair_step,
        [
            right_blocks, left_t, left_p, pair_p, cot_p, back, out_weight, trans_up,
            in_hbm(ln_gain.reshape(1, dim)), in_hbm(out_bias.reshape(1, dim)),
        ],
        [
            ((SEQS // 2, right_size), BF16),
            ((SEQS // 2, right_size), F32),
            ((cells, dim), F32),
            ((cells, ffn), BF16),
            ((SEQS, left_size), BF16),
        ],
        [
            ((max(left_size, cells), max(right_size, C * C)), F32),
            ((cells, C * C), BF16),
            ((SEQS, right_size), BF16),
            ((left_size, right_size), BF16),
            ((SEQS, left_size), BF16),
            ((1, dim), F32),
            ((1, dim), F32),
            pltpu.SemaphoreType.DMA((3,)),
        ],
        far_in=2,
        far_out=1,
    )
    came = lax.ppermute(away, "row", [(k, (k + half) % owners) for k in range(owners)])
    left_tiles = to_each(grad_left.reshape(-1, *left.shape), "col")
    (tiles,) = on_core(
        join_halves, [kept, came], [((half, *right.shape), BF16)], [((SEQS // 2, right_size), F32)]
    )
    right_tiles = to_each(tiles, "row", back_order)
    (pair_out,) = on_core(finish, [middle, hidden, trans_down], [(pair_in.shape, BF16)])
    (grad_left,) = on_core(left_sum, [left_tiles], [(left.shape, BF16)])
    (grad_right,) = on_core(right_sum, [right_tiles], [(right.shape, BF16)])
    return pair_out, grad_left, grad_right


def solution(mesh):
    return jax.shard_map(
        on_device,
        mesh=mesh,
        in_specs=(
            P("col", "row"),
            P("row", "col"),
            P("row", "col", None),
            P("row", "col", None),
            P(),
            P(),
            P(),
            P(),
            P(),
        ),
        out_specs=(P("row", "col", None), P("col", "row"), P("row", "col")),
        check_vma=False,
    )
```

```python
import jax
import jax.numpy as jnp
from jax import lax
from jax.experimental import pallas as pl
from jax.experimental.pallas import tpu as pltpu
from jax.sharding import PartitionSpec as P

C = 32
SEQS = 128
GROUPS = 128 // C
F32 = jnp.float32
BF16 = jnp.bfloat16
Y, X, CORES = 4, 2, 2
OUT, BACK = (11, 7), (9, 7)
NN = (((1,), (0,)), ((), ()))
NT = (((1,), (1,)), ((), ()))
TN = (((0,), (0,)), ((), ()))


def mm(a, b, dims=NN):
    return lax.dot_general(a, b, dims, preferred_element_type=F32)


def swap_rows(major, minor):
    n = major * minor
    row = lax.broadcasted_iota(jnp.int32, (n, n), 0)
    col = lax.broadcasted_iota(jnp.int32, (n, n), 1)
    return jnp.where(col == (row % minor) * major + row // minor, 1.0, 0.0).astype(BF16)


def exchange(tiles):
    axis = tiles[0].ndim - 1
    lane = lax.broadcasted_iota(jnp.int32, tiles[0].shape, axis)
    low, even = lane < 64, lane % 64 < 32
    a0, a1, a2, a3 = tiles
    b0, b2 = jnp.where(low, a0, pltpu.roll(a2, 64, axis)), jnp.where(low, pltpu.roll(a0, 64, axis), a2)
    b1, b3 = jnp.where(low, a1, pltpu.roll(a3, 64, axis)), jnp.where(low, pltpu.roll(a1, 64, axis), a3)
    c0, c1 = jnp.where(even, b0, pltpu.roll(b1, 32, axis)), jnp.where(even, pltpu.roll(b0, 96, axis), b1)
    c2, c3 = jnp.where(even, b2, pltpu.roll(b3, 32, axis)), jnp.where(even, pltpu.roll(b2, 96, axis), b3)
    return c0, c1, c2, c3


def regroup(src, dst, rows, scale=None):
    for g in range(src.shape[0] // (GROUPS * rows)):
        for h in range(src.shape[1] // 128):
            tiles = [
                src[(GROUPS * g + t) * rows : (GROUPS * g + t + 1) * rows, h * 128 : (h + 1) * 128]
                for t in range(GROUPS)
            ]
            if scale is not None:
                tiles = [tile * scale for tile in tiles]
            tiles = [tile.astype(BF16) for tile in tiles]
            for t, tile in enumerate(exchange(tiles)):
                at = (GROUPS * h + t) * rows
                dst[at : at + rows, g * 128 : (g + 1) * 128] = tile


def prepare(left, pair_in, pair_cot, down, left_t, left_p, pair_p, cot_p, back):
    rows, cols, _ = pair_in.shape
    swap = swap_rows(C, rows)
    swap_pair = swap if cols == C else swap_rows(cols, rows)
    ring = chip_ring()
    each = left.shape[0] // len(ring)
    came = left[...].astype(F32)
    blocks = [came[ring.index(k) * each : (ring.index(k) + 1) * each] for k in range(len(ring))]
    left_all = jnp.concatenate(blocks, axis=0).astype(BF16)
    left_t[...] = mm(swap, left_all, NT).astype(BF16)
    left_p[...] = mm(left_all, swap, NT).astype(BF16)
    pair_p[...] = mm(swap_pair, pair_in[...].reshape(rows * cols, -1)).astype(BF16)
    cot = mm(swap_pair, pair_cot[...].reshape(rows * cols, -1)).astype(BF16)
    cot_p[...] = cot
    back[...] = mm(cot, down[...], NT).astype(BF16)


def chip_ring():
    chips = [(y, 0) for y in range(Y)] + [(y, 1) for y in reversed(range(Y))]
    return [(y * X + x) * CORES + core for y, x in chips for core in range(CORES)]


def listed(count, order):
    first, stride = order
    return [(first + stride * k) % count for k in range(count)]


def pair_step(
    right, left_t, left_p, pair_p, cot_p, back, weight, up, gain_in, bias_in,
    away, kept, middle_out, hidden_out, grad_left,
    tall, outer, right_all, d_tiles, partial, gain, bias, sems,
):
    fetch_gain = pltpu.make_async_copy(gain_in, gain, sems.at[0])
    fetch_bias = pltpu.make_async_copy(bias_in, bias, sems.at[1])
    fetch_gain.start()
    fetch_bias.start()
    owners, each, width = right.shape
    rows = left_t.shape[0] // C
    for k, z in enumerate(listed(owners // 2, OUT)):
        for at, block in ((z, 2 * k), (z + owners // 2, 2 * k + 1)):
            tall[at * each : (at + 1) * each, :] = right[block].astype(F32)
    right_all[...] = tall[: owners * each, :].astype(BF16)
    tall[...] = mm(left_t[...], right_all[...])
    regroup(tall, outer, rows, 1.0 / SEQS)
    update = mm(outer[...], weight[...])
    fetch_gain.wait()
    fetch_bias.wait()
    middle = pair_p[...].astype(F32) + update + bias[...]
    middle_out[...] = middle
    centre = jnp.mean(middle, axis=-1, keepdims=True)
    centred = middle - centre
    spread = jnp.mean(centred * centred, axis=-1, keepdims=True)
    inverse = lax.rsqrt(spread + 1e-05)
    normal_x = centred * inverse
    normed = (normal_x * gain[...]).astype(BF16)
    preact = mm(normed, up[...])
    hidden_out[...] = jnp.maximum(preact, 0.0).astype(BF16)
    d_hidden = jnp.where(preact > 0.0, back[...].astype(F32), 0.0).astype(BF16)
    scaled = mm(d_hidden, up[...], NT) * gain[...]
    d_middle = cot_p[...].astype(F32) + inverse * (
        scaled
        - jnp.mean(scaled, axis=-1, keepdims=True)
        - normal_x * jnp.mean(scaled * normal_x, axis=-1, keepdims=True)
    )
    tall[...] = mm(d_middle.astype(BF16), weight[...], NT)
    regroup(tall, d_tiles, rows)
    partial[...] = mm(right_all[...], d_tiles[...], NT).astype(BF16)
    send = pltpu.make_async_copy(partial, grad_left, sems.at[2])
    send.start()
    half = SEQS // 2
    mine = lax.axis_index("row") // (owners // 2)
    away[...] = mm(left_p[pl.ds((1 - mine) * half, half), :], d_tiles[...]).astype(BF16)
    kept[...] = mm(left_p[pl.ds(mine * half, half), :], d_tiles[...])
    send.wait()


def left_sum(arrived, grad_left):
    total = jnp.sum(arrived[...].astype(F32), axis=0)
    mine = (total * (1.0 / SEQS)).astype(BF16)
    grad_left[...] = mm(mine, swap_rows(C, grad_left.shape[1] // C)).astype(BF16)


def right_sum(arrived, grad_right):
    total = jnp.sum(arrived[...].astype(F32), axis=0)
    grad_right[...] = (total * (1.0 / SEQS)).astype(BF16)


def join_halves(kept, came, tiles, total):
    owners, each, _ = tiles.shape
    total[...] = kept[...] + came[...].astype(F32)
    for k, z in enumerate(listed(owners, BACK)):
        tiles[k] = total[z * each : (z + 1) * each, :].astype(BF16)


def finish(middle, hidden, down, pair_out):
    rows, cols, _ = pair_out.shape
    swap_pair = swap_rows(cols, rows)
    out = (middle[...] + mm(hidden[...], down[...])).astype(BF16)
    pair_out[...] = mm(swap_pair, out, TN).astype(BF16).reshape(pair_out.shape)


def in_hbm(x):
    return pltpu.with_memory_space_constraint(x, pltpu.HBM)


VMEM = pl.BlockSpec(memory_space=pltpu.VMEM)
HBM = pl.BlockSpec(memory_space=pltpu.HBM)


def on_core(kernel, args, outs, scratch=(), far_in=0, far_out=0):
    return pl.pallas_call(
        kernel,
        out_shape=[jax.ShapeDtypeStruct(*out) for out in outs],
        in_specs=[VMEM] * (len(args) - far_in) + [HBM] * far_in,
        out_specs=[VMEM] * (len(outs) - far_out) + [HBM] * far_out,
        scratch_shapes=[pltpu.VMEM(*s) if isinstance(s, tuple) else s for s in scratch],
        compiler_params=pltpu.CompilerParams(vmem_limit_bytes=32 << 20),
        cost_estimate=pl.CostEstimate(
            flops=400_000_000, bytes_accessed=2_000_000, transcendentals=0
        ),
    )(*args)


def to_each(tiles, axis, groups=None):
    return lax.all_to_all(
        tiles, axis, split_axis=0, concat_axis=0, tiled=True, axis_index_groups=groups
    )


def on_device(left, right, pair_in, pair_cot, ln_gain, out_weight, out_bias, trans_up, trans_down):
    rows, cols, dim = pair_in.shape
    cells, ffn = rows * cols, trans_up.shape[1]
    left_size, right_size = rows * C, cols * C
    owners = lax.axis_size("row")
    half = owners // 2
    out_order, back_order = (
        [[start + z for z in listed(half, order)] for start in (0, half)] for order in (OUT, BACK)
    )
    copies = jnp.broadcast_to(right, (owners, *right.shape))
    right_blocks = to_each(copies, "row", [[k for pair in zip(*out_order) for k in pair]])
    left_blocks = lax.all_gather(
        left, "col", axis=0, tiled=True, axis_index_groups=[chip_ring()]
    )
    left_t, left_p, pair_p, cot_p, back = on_core(
        prepare,
        [left_blocks, pair_in, pair_cot, trans_down],
        [
            ((left_size, SEQS), BF16),
            ((SEQS, left_size), BF16),
            ((cells, dim), BF16),
            ((cells, dim), BF16),
            ((cells, ffn), BF16),
        ],
    )
    away, kept, middle, hidden, grad_left = on_core(
        pair_step,
        [
            right_blocks, left_t, left_p, pair_p, cot_p, back, out_weight, trans_up,
            in_hbm(ln_gain.reshape(1, dim)), in_hbm(out_bias.reshape(1, dim)),
        ],
        [
            ((SEQS // 2, right_size), BF16),
            ((SEQS // 2, right_size), F32),
            ((cells, dim), F32),
            ((cells, ffn), BF16),
            ((SEQS, left_size), BF16),
        ],
        [
            ((max(left_size, cells), max(right_size, C * C)), F32),
            ((cells, C * C), BF16),
            ((SEQS, right_size), BF16),
            ((left_size, right_size), BF16),
            ((SEQS, left_size), BF16),
            ((1, dim), F32),
            ((1, dim), F32),
            pltpu.SemaphoreType.DMA((3,)),
        ],
        far_in=2,
        far_out=1,
    )
    came = lax.ppermute(away, "row", [(k, (k + half) % owners) for k in range(owners)])
    left_tiles = to_each(grad_left.reshape(-1, *left.shape), "col")
    (tiles,) = on_core(
        join_halves, [kept, came], [((half, *right.shape), BF16)], [((SEQS // 2, right_size), F32)]
    )
    right_tiles = to_each(tiles, "row", back_order)
    (pair_out,) = on_core(finish, [middle, hidden, trans_down], [(pair_in.shape, BF16)])
    (grad_left,) = on_core(left_sum, [left_tiles], [(left.shape, BF16)])
    (grad_right,) = on_core(right_sum, [right_tiles], [(right.shape, BF16)])
    return pair_out, grad_left, grad_right


def solution(mesh):
    return jax.shard_map(
        on_device,
        mesh=mesh,
        in_specs=(
            P("col", "row"),
            P("row", "col"),
            P("row", "col", None),
            P("row", "col", None),
            P(),
            P(),
            P(),
            P(),
            P(),
        ),
        out_specs=(P("row", "col", None), P("col", "row"), P("row", "col")),
        check_vma=False,
    )
```

```python
import jax
import jax.numpy as jnp
from jax import lax
from jax.experimental import pallas as pl
from jax.experimental.pallas import tpu as pltpu
from jax.sharding import PartitionSpec as P

C = 32
SEQS = 128
GROUPS = 128 // C
F32 = jnp.float32
BF16 = jnp.bfloat16
Y, X, CORES = 4, 2, 2
OUT, BACK = (11, 7), (9, 7)
NN = (((1,), (0,)), ((), ()))
NT = (((1,), (1,)), ((), ()))
TN = (((0,), (0,)), ((), ()))


def mm(a, b, dims=NN):
    return lax.dot_general(a, b, dims, preferred_element_type=F32)


def swap_rows(major, minor):
    n = major * minor
    row = lax.broadcasted_iota(jnp.int32, (n, n), 0)
    col = lax.broadcasted_iota(jnp.int32, (n, n), 1)
    return jnp.where(col == (row % minor) * major + row // minor, 1.0, 0.0).astype(BF16)


def exchange(tiles):
    axis = tiles[0].ndim - 1
    lane = lax.broadcasted_iota(jnp.int32, tiles[0].shape, axis)
    low, even = lane < 64, lane % 64 < 32
    a0, a1, a2, a3 = tiles
    b0, b2 = jnp.where(low, a0, pltpu.roll(a2, 64, axis)), jnp.where(low, pltpu.roll(a0, 64, axis), a2)
    b1, b3 = jnp.where(low, a1, pltpu.roll(a3, 64, axis)), jnp.where(low, pltpu.roll(a1, 64, axis), a3)
    c0, c1 = jnp.where(even, b0, pltpu.roll(b1, 32, axis)), jnp.where(even, pltpu.roll(b0, 96, axis), b1)
    c2, c3 = jnp.where(even, b2, pltpu.roll(b3, 32, axis)), jnp.where(even, pltpu.roll(b2, 96, axis), b3)
    return c0, c1, c2, c3


def regroup(src, dst, rows, scale=None):
    for g in range(src.shape[0] // (GROUPS * rows)):
        for h in range(src.shape[1] // 128):
            tiles = [
                src[(GROUPS * g + t) * rows : (GROUPS * g + t + 1) * rows, h * 128 : (h + 1) * 128]
                for t in range(GROUPS)
            ]
            if scale is not None:
                tiles = [tile * scale for tile in tiles]
            tiles = [tile.astype(BF16) for tile in tiles]
            for t, tile in enumerate(exchange(tiles)):
                at = (GROUPS * h + t) * rows
                dst[at : at + rows, g * 128 : (g + 1) * 128] = tile


def prepare(left, pair_in, pair_cot, down, left_t, left_p, pair_p, cot_p, back):
    rows, cols, _ = pair_in.shape
    swap = swap_rows(C, rows)
    swap_pair = swap if cols == C else swap_rows(cols, rows)
    left_t[...] = mm(swap, left[...], NT).astype(BF16)
    ring = chip_ring()
    each = left.shape[0] // len(ring)
    turned = mm(left[...], swap, NT)
    blocks = [turned[ring.index(k) * each : (ring.index(k) + 1) * each] for k in range(len(ring))]
    left_p[...] = jnp.concatenate(blocks, axis=0).astype(BF16)
    pair_p[...] = mm(swap_pair, pair_in[...].reshape(rows * cols, -1)).astype(BF16)
    cot = mm(swap_pair, pair_cot[...].reshape(rows * cols, -1)).astype(BF16)
    cot_p[...] = cot
    back[...] = mm(cot, down[...], NT).astype(BF16)


def chip_ring():
    chips = [(y, 0) for y in range(Y)] + [(y, 1) for y in reversed(range(Y))]
    return [(y * X + x) * CORES + core for y, x in chips for core in range(CORES)]


def listed(count, order):
    first, stride = order
    return [(first + stride * k) % count for k in range(count)]


def pair_step(
    right, left_t, left_p, pair_p, cot_p, back, weight, up, gain_in, bias_in,
    away, kept, middle_out, hidden_out, grad_left,
    tall, outer, right_all, d_tiles, partial, gain, bias, sems,
):
    fetch_gain = pltpu.make_async_copy(gain_in, gain, sems.at[0])
    fetch_bias = pltpu.make_async_copy(bias_in, bias, sems.at[1])
    fetch_gain.start()
    fetch_bias.start()
    owners, each, width = right.shape
    rows = left_t.shape[0] // C
    ring = chip_ring()
    share = owners // len(ring)
    for k, z in enumerate(listed(owners // 2, OUT)):
        for at, block in ((z, 2 * k), (z + owners // 2, 2 * k + 1)):
            row = ring.index(at // share) * share * each + at % share * each
            tall[row : row + each, :] = right[block].astype(F32)
    right_all[...] = tall[: owners * each, :].astype(BF16)
    tall[...] = mm(left_t[...], right_all[...])
    regroup(tall, outer, rows, 1.0 / SEQS)
    update = mm(outer[...], weight[...])
    fetch_gain.wait()
    fetch_bias.wait()
    middle = pair_p[...].astype(F32) + update + bias[...]
    middle_out[...] = middle
    centre = jnp.mean(middle, axis=-1, keepdims=True)
    centred = middle - centre
    spread = jnp.mean(centred * centred, axis=-1, keepdims=True)
    inverse = lax.rsqrt(spread + 1e-05)
    normal_x = centred * inverse
    normed = (normal_x * gain[...]).astype(BF16)
    preact = mm(normed, up[...])
    hidden_out[...] = jnp.maximum(preact, 0.0).astype(BF16)
    d_hidden = jnp.where(preact > 0.0, back[...].astype(F32), 0.0).astype(BF16)
    scaled = mm(d_hidden, up[...], NT) * gain[...]
    d_middle = cot_p[...].astype(F32) + inverse * (
        scaled
        - jnp.mean(scaled, axis=-1, keepdims=True)
        - normal_x * jnp.mean(scaled * normal_x, axis=-1, keepdims=True)
    )
    tall[...] = mm(d_middle.astype(BF16), weight[...], NT)
    regroup(tall, d_tiles, rows)
    partial[...] = mm(right_all[...], d_tiles[...], NT).astype(BF16)
    send = pltpu.make_async_copy(partial, grad_left, sems.at[2])
    send.start()
    half = SEQS // 2
    mine = lax.axis_index("row") // (owners // 2)
    away[...] = mm(left_p[pl.ds((1 - mine) * half, half), :], d_tiles[...]).astype(BF16)
    kept[...] = mm(left_p[pl.ds(mine * half, half), :], d_tiles[...])
    send.wait()


def left_sum(arrived, grad_left):
    total = jnp.sum(arrived[...].astype(F32), axis=0)
    mine = (total * (1.0 / SEQS)).astype(BF16)
    grad_left[...] = mm(mine, swap_rows(C, grad_left.shape[1] // C)).astype(BF16)


def right_sum(arrived, grad_right):
    total = jnp.sum(arrived[...].astype(F32), axis=0)
    grad_right[...] = (total * (1.0 / SEQS)).astype(BF16)


def join_halves(kept, came, tiles, total):
    owners, each, _ = tiles.shape
    total[...] = kept[...] + came[...].astype(F32)
    for k, z in enumerate(listed(owners, BACK)):
        tiles[k] = total[z * each : (z + 1) * each, :].astype(BF16)


def finish(middle, hidden, down, pair_out):
    rows, cols, _ = pair_out.shape
    swap_pair = swap_rows(cols, rows)
    out = (middle[...] + mm(hidden[...], down[...])).astype(BF16)
    pair_out[...] = mm(swap_pair, out, TN).astype(BF16).reshape(pair_out.shape)


def in_hbm(x):
    return pltpu.with_memory_space_constraint(x, pltpu.HBM)


VMEM = pl.BlockSpec(memory_space=pltpu.VMEM)
HBM = pl.BlockSpec(memory_space=pltpu.HBM)


def on_core(kernel, args, outs, scratch=(), far_in=0, far_out=0):
    return pl.pallas_call(
        kernel,
        out_shape=[jax.ShapeDtypeStruct(*out) for out in outs],
        in_specs=[VMEM] * (len(args) - far_in) + [HBM] * far_in,
        out_specs=[VMEM] * (len(outs) - far_out) + [HBM] * far_out,
        scratch_shapes=[pltpu.VMEM(*s) if isinstance(s, tuple) else s for s in scratch],
        compiler_params=pltpu.CompilerParams(vmem_limit_bytes=32 << 20),
        cost_estimate=pl.CostEstimate(
            flops=400_000_000, bytes_accessed=2_000_000, transcendentals=0
        ),
    )(*args)


def to_each(tiles, axis, groups=None):
    return lax.all_to_all(
        tiles, axis, split_axis=0, concat_axis=0, tiled=True, axis_index_groups=groups
    )


def on_device(left, right, pair_in, pair_cot, ln_gain, out_weight, out_bias, trans_up, trans_down):
    rows, cols, dim = pair_in.shape
    cells, ffn = rows * cols, trans_up.shape[1]
    left_size, right_size = rows * C, cols * C
    owners = lax.axis_size("row")
    half = owners // 2
    out_order, back_order = (
        [[start + z for z in listed(half, order)] for start in (0, half)] for order in (OUT, BACK)
    )
    copies = jnp.broadcast_to(right, (owners, *right.shape))
    right_blocks = to_each(copies, "row", [[k for pair in zip(*out_order) for k in pair]])
    left_blocks = lax.all_gather(
        left, "col", axis=0, tiled=True, axis_index_groups=[chip_ring()]
    )
    left_t, left_p, pair_p, cot_p, back = on_core(
        prepare,
        [left_blocks, pair_in, pair_cot, trans_down],
        [
            ((left_size, SEQS), BF16),
            ((SEQS, left_size), BF16),
            ((cells, dim), BF16),
            ((cells, dim), BF16),
            ((cells, ffn), BF16),
        ],
    )
    away, kept, middle, hidden, grad_left = on_core(
        pair_step,
        [
            right_blocks, left_t, left_p, pair_p, cot_p, back, out_weight, trans_up,
            in_hbm(ln_gain.reshape(1, dim)), in_hbm(out_bias.reshape(1, dim)),
        ],
        [
            ((SEQS // 2, right_size), BF16),
            ((SEQS // 2, right_size), F32),
            ((cells, dim), F32),
            ((cells, ffn), BF16),
            ((SEQS, left_size), BF16),
        ],
        [
            ((max(left_size, cells), max(right_size, C * C)), F32),
            ((cells, C * C), BF16),
            ((SEQS, right_size), BF16),
            ((left_size, right_size), BF16),
            ((SEQS, left_size), BF16),
            ((1, dim), F32),
            ((1, dim), F32),
            pltpu.SemaphoreType.DMA((3,)),
        ],
        far_in=2,
        far_out=1,
    )
    came = lax.ppermute(away, "row", [(k, (k + half) % owners) for k in range(owners)])
    left_tiles = to_each(grad_left.reshape(-1, *left.shape), "col", [chip_ring()])
    (tiles,) = on_core(
        join_halves, [kept, came], [((half, *right.shape), BF16)], [((SEQS // 2, right_size), F32)]
    )
    right_tiles = to_each(tiles, "row", back_order)
    (pair_out,) = on_core(finish, [middle, hidden, trans_down], [(pair_in.shape, BF16)])
    (grad_left,) = on_core(left_sum, [left_tiles], [(left.shape, BF16)])
    (grad_right,) = on_core(right_sum, [right_tiles], [(right.shape, BF16)])
    return pair_out, grad_left, grad_right


def solution(mesh):
    return jax.shard_map(
        on_device,
        mesh=mesh,
        in_specs=(
            P("col", "row"),
            P("row", "col"),
            P("row", "col", None),
            P("row", "col", None),
            P(),
            P(),
            P(),
            P(),
            P(),
        ),
        out_specs=(P("row", "col", None), P("col", "row"), P("row", "col")),
        check_vma=False,
    )
```
